32 devices in a mesh: dp: 16 (over z, y, x), tensor: 2 (over core).
Axes of the slice: x: 2, y: 2, z: 4, core: 2. Of those that a mesh axis runs over, the one named last changes fastest.
Arguments:
- tokens: bfloat16 [8192, 768], P('dp', 'tensor'), may hold values from -6 to 6
- segment: int32 [8192], P('dp'), may hold values from 0 to 3, as said below
- first_norm_scale: float32 [768], replicated, may hold values from 0.5 to 2
- first_norm_bias: float32 [768], replicated, may hold values from -3 to 3
- w_qkv: bfloat16 [768, 3, 768], P(None, None, 'tensor'), may hold values from -2.5 to 2.5
- q_bias: float32 [768], P('tensor'), may hold values from -3 to 3
- v_bias: float32 [768], P('tensor'), may hold values from -3 to 3
- w_o: bfloat16 [768, 768], P('tensor'), may hold values from -0.875 to 0.875
- o_bias: float32 [768], replicated, may hold values from -3 to 3
- second_norm_scale: float32 [768], replicated, may hold values from 0.5 to 2
- second_norm_bias: float32 [768], replicated, may hold values from -3 to 3
- w_fc: bfloat16 [768, 3072], P(None, 'tensor'), may hold values from -0.21875 to 0.21875
- fc_bias: float32 [3072], P('tensor'), may hold values from -3 to 3
- w_pr: bfloat16 [3072, 768], P('tensor'), may hold values from -0.109375 to 0.109375
- pr_bias: float32 [768], replicated, may hold values from -3 to 3
- cotangent: bfloat16 [8192, 768], P('dp', 'tensor'), may hold values from -6 to 6
Outputs:
- block_out: bfloat16 [8192, 768], P('dp', 'tensor')
- grad_tokens: float32 [8192, 768], P('dp', 'tensor')
- grad_ln1_gain: float32 [768], P(('tensor', 'dp'))
- grad_ln1_bias: float32 [768], P(('tensor', 'dp'))
- grad_w_qkv: float32 [768, 3, 768], P('dp', None, 'tensor')
- grad_q_bias: float32 [768], P(('tensor', 'dp'))
- grad_v_bias: float32 [768], P(('tensor', 'dp'))
- grad_w_o: float32 [768, 768], P(('tensor', 'dp'))
- grad_o_bias: float32 [768], P('dp')
- grad_ln2_gain: float32 [768], P('dp')
- grad_ln2_bias: float32 [768], P('dp')
- grad_w_fc: float32 [768, 3072], P('dp', 'tensor')
- grad_fc_bias: float32 [3072], P(('tensor', 'dp'))
- grad_w_pr: float32 [3072, 768], P(('tensor', 'dp'))
- grad_pr_bias: float32 [768], P('dp')
The draws below stay inside these ranges and needn't reach their ends.
Inputs may be any that keep to these rules, and one draw needn't show every extreme that they name: `segment`: within each aligned block of 512 rows the ids start at 0 and never fall; equal ids in a block form one causal sequence. Some block holds four sequences and some block is one sequence of 512 rows.
All inputs are finite; a program needn't handle non-finite values.
Results may differ from the reference program's by a relative error of at most 0.015.
Values may be sent and summed in bfloat16 or wider, within the bound.
A program may use at most 128 MiB of HBM per device.

```python
import math
import jax
import jax.numpy as jnp
from jax import lax

D = 768
HEADS = 12
HEAD = 64
FF = 3072
CAP = 512
TOKENS = 8192
N_DP = 16


def draw_segment(key, part):
    blocks = TOKENS // CAP
    key_cuts, key_keep = jax.random.split(key, 2)
    cuts = jax.random.randint(key_cuts, (blocks, 3), 1, CAP)
    enable = jax.random.randint(key_keep, (blocks, 3), 0, 2)
    block_ids = jnp.arange(blocks)[:, None]
    enable = jnp.where(block_ids == 0, 1, jnp.where(block_ids == 1, 0, enable))
    position = jnp.arange(CAP)
    passed = (position[None, :, None] >= cuts[:, None, :]).astype(jnp.int32)
    seg_ids = jnp.sum(passed * enable[:, None, :], axis=2)
    return seg_ids.reshape(TOKENS).astype(jnp.int32)


def draw_w_qkv(key, part):
    key_base = jax.random.fold_in(key, 0)
    base = jnp.clip(jax.random.normal(key_base, (D, 3, D), jnp.float32), -5.0, 5.0) / math.sqrt(D)
    return base.astype(jnp.bfloat16)


def with_spikes(result, rng, source, target, blocks, factor):
    def block_of(dim):
        return (jnp.arange(result.shape[dim]) // (result.shape[dim] // blocks)).reshape((-1,) + (1,) * (result.ndim - 1 - dim))

    first = jax.random.permutation(rng, blocks)[block_of(target)]
    far = (block_of(target) + blocks // 2) % blocks
    return jnp.where((block_of(source) == first) | (block_of(source) == far), factor * result, result)


def block_levels(key, extent, cuts, low, high):
    level = 1.0
    for dim, shards_of in cuts:
        heights = jax.random.uniform(jax.random.fold_in(jax.random.fold_in(key, 6), dim), (shards_of,), jnp.float32, low / len(cuts), high / len(cuts))
        level = level * jnp.repeat(jnp.exp(heights), extent[dim] // shards_of).reshape((-1,) + (1,) * (len(extent) - 1 - dim))
    return level


def gaussian(own_key, shape, spread, bound, cuts=(), kind=jnp.bfloat16):
    loudness = block_levels(own_key, shape, cuts, -0.22, 0.18) if cuts else 1.0
    drawn = jax.random.normal(own_key, shape, jnp.float32) * spread * loudness
    return jnp.minimum(jnp.maximum(drawn, -bound), bound).astype(kind)


def bell_draw_with(own_key, extent, scale, limit, cuts, heavy, dtype=jnp.bfloat16):
    values = scale * jax.random.normal(own_key, extent, jnp.float32)
    if cuts:
        values = values * block_levels(own_key, extent, cuts, -0.22, 0.18)
    return jnp.clip(with_spikes(values, jax.random.fold_in(own_key, 3), *heavy), -limit, limit).astype(dtype)


def setup_inputs(seed: int = 0) -> dict:
    splits = jax.random.split(jax.random.key(seed), 17)
    tokens = gaussian(splits[0], (TOKENS, D), 1.0, 6.0, ((0, 16), (1, 2)))
    segment = draw_segment(jax.random.fold_in(splits[16], 71), 0)
    first_norm_scale = jnp.clip(jnp.exp(jax.random.uniform(splits[2], (D,), jnp.float32, math.log(0.5), math.log(2.0))), 0.5, 2.0)
    first_norm_bias = gaussian(splits[3], (D,), 0.5, 3.0, (), jnp.float32)
    w_qkv = draw_w_qkv(jax.random.fold_in(splits[16], 71), 0)
    q_bias = gaussian(splits[5], (D,), 0.5, 3.0, ((0, 2),), jnp.float32)
    v_bias = gaussian(splits[6], (D,), 0.5, 3.0, ((0, 2),), jnp.float32)
    w_o = gaussian(splits[7], (D, D), (D // 16) ** -0.5, 0.875, ((0, 2),))
    o_bias = gaussian(splits[8], (D,), 0.5, 3.0, (), jnp.float32)
    second_norm_scale = jnp.clip(jnp.exp(jax.random.uniform(splits[9], (D,), jnp.float32, math.log(0.5), math.log(2.0))), 0.5, 2.0)
    second_norm_bias = gaussian(splits[10], (D,), 0.5, 3.0, (), jnp.float32)
    w_fc = gaussian(splits[11], (D, FF), D ** -0.5, 0.21875, ((1, 2),))
    fc_bias = gaussian(splits[12], (FF,), 0.5, 3.0, ((0, 2),), jnp.float32)
    w_pr = gaussian(splits[13], (FF, D), FF ** -0.5, 0.109375, ((0, 2),))
    pr_bias = gaussian(splits[14], (D,), 0.5, 3.0, (), jnp.float32)
    cotangent = bell_draw_with(splits[15], (TOKENS, D), 1.0, 6.0, ((0, 16), (1, 2)), (0, 1, 16, 2.0))
    return {"tokens": tokens, "segment": segment, "first_norm_scale": first_norm_scale, "first_norm_bias": first_norm_bias, "w_qkv": w_qkv, "q_bias": q_bias, "v_bias": v_bias, "w_o": w_o, "o_bias": o_bias, "second_norm_scale": second_norm_scale, "second_norm_bias": second_norm_bias, "w_fc": w_fc, "fc_bias": fc_bias, "w_pr": w_pr, "pr_bias": pr_bias, "cotangent": cotangent}


gelu_cubic = 0.044715
root_two_pi = math.sqrt(2.0 / math.pi)

def apply_layer_norm(residual_stream):
    center = residual_stream - lax.optimization_barrier(jnp.mean(residual_stream, axis=-1, keepdims=True))
    inverse_deviation = lax.rsqrt(lax.optimization_barrier(jnp.mean(center * center, axis=-1, keepdims=True)) + 1e-05)
    return (center * inverse_deviation, inverse_deviation)

def norm_gradient(centered_gradient, normalized_input, inverse_deviation):
    return inverse_deviation * (centered_gradient - lax.optimization_barrier(jnp.mean(centered_gradient, axis=-1, keepdims=True)) - normalized_input * lax.optimization_barrier(jnp.mean(centered_gradient * normalized_input, axis=-1, keepdims=True)))

def gelu_value(pre):
    inner = root_two_pi * (pre + gelu_cubic * pre * pre * pre)
    return 0.5 * pre * (1.0 + jnp.tanh(inner))

def gelu_slope(pre):
    tanh_val = jnp.tanh(root_two_pi * (pre + gelu_cubic * pre * pre * pre))
    return 0.5 * (1.0 + tanh_val) + 0.5 * pre * (1.0 - tanh_val * tanh_val) * root_two_pi * (1.0 + 3.0 * gelu_cubic * pre * pre)

def allowed_pairs(segment, begin_row, block_rows):
    query_pos = begin_row + jnp.arange(block_rows)
    key_pos = jnp.arange(segment.shape[0])
    same = segment[begin_row:begin_row + block_rows][:, None] == segment[None, :]
    return same & (key_pos[None, :] <= query_pos[:, None])

def score_block(query_blk, key_heads, allowed, score_scale):
    scores = jnp.einsum('qhe,khe->hqk', query_blk.astype(jnp.float32), key_heads.astype(jnp.float32)) * score_scale
    return jnp.where(allowed[None], scores, -1e+30)

def attend(queries, keys_in, vals_in, segment):
    rows_all = queries.shape[0]
    query_h = queries.reshape(rows_all, HEADS, HEAD)
    key_h = keys_in.reshape(rows_all, HEADS, HEAD)
    val_h = vals_in.reshape(rows_all, HEADS, HEAD)
    block_rows = min(512, rows_all)
    score_scale = 1.0 / math.sqrt(HEAD)
    outputs = []
    totals = []
    for begin_row in range(0, rows_all, block_rows):
        allowed = allowed_pairs(segment, begin_row, block_rows)
        scores = score_block(query_h[begin_row:begin_row + block_rows], key_h, allowed, score_scale)
        row_max = lax.optimization_barrier(jnp.max(scores, axis=-1, keepdims=True))
        raw = jnp.exp(scores - row_max)
        row_total = lax.optimization_barrier(jnp.sum(raw, axis=-1, keepdims=True))
        probs = (raw / row_total).astype(jnp.bfloat16)
        mixed_part = jnp.einsum('hqk,khe->qhe', probs.astype(jnp.float32), val_h.astype(jnp.float32)).astype(jnp.bfloat16)
        outputs.append(mixed_part.reshape(block_rows, HEADS * HEAD))
        totals.append((row_max + jnp.log(row_total))[..., 0])
    return (jnp.concatenate(outputs, axis=0), jnp.concatenate(totals, axis=1))

def attend_back(queries, keys_in, vals_in, att, grad_att, lse, segment):
    rows_all = queries.shape[0]
    query_h = queries.reshape(rows_all, HEADS, HEAD)
    key_h = keys_in.reshape(rows_all, HEADS, HEAD)
    val_h = vals_in.reshape(rows_all, HEADS, HEAD)
    att_h = att.reshape(rows_all, HEADS, HEAD)
    grad_h = grad_att.reshape(rows_all, HEADS, HEAD)
    block_rows = min(512, rows_all)
    score_scale = 1.0 / math.sqrt(HEAD)
    grad_key_sum = jnp.zeros((rows_all, HEADS, HEAD), jnp.float32)
    grad_val_sum = jnp.zeros((rows_all, HEADS, HEAD), jnp.float32)
    query_parts = []
    for begin_row in range(0, rows_all, block_rows):
        allowed = allowed_pairs(segment, begin_row, block_rows)
        query_blk = query_h[begin_row:begin_row + block_rows]
        scores = score_block(query_blk, key_h, allowed, score_scale)
        probs_f = jnp.exp(scores - lse[:, begin_row:begin_row + block_rows, None])
        probs_b = probs_f.astype(jnp.bfloat16)
        grad_blk = grad_h[begin_row:begin_row + block_rows]
        att_blk = att_h[begin_row:begin_row + block_rows]
        grad_val_sum = grad_val_sum + jnp.einsum('hqk,qhe->khe', probs_b.astype(jnp.float32), grad_blk.astype(jnp.float32))
        dprob = jnp.einsum('qhe,khe->hqk', grad_blk.astype(jnp.float32), val_h.astype(jnp.float32))
        delta = lax.optimization_barrier(jnp.sum(grad_blk.astype(jnp.float32) * att_blk.astype(jnp.float32), axis=-1)).T
        grad_score = (probs_f * (dprob - delta[:, :, None])).astype(jnp.bfloat16)
        query_parts.append((jnp.einsum('hqk,khe->qhe', grad_score.astype(jnp.float32), key_h.astype(jnp.float32)) * score_scale).reshape(block_rows, HEADS * HEAD))
        grad_key_sum = grad_key_sum + jnp.einsum('hqk,qhe->khe', grad_score.astype(jnp.float32), query_blk.astype(jnp.float32)) * score_scale
    return (jnp.concatenate(query_parts, axis=0), grad_key_sum.reshape(rows_all, HEADS * HEAD), grad_val_sum.reshape(rows_all, HEADS * HEAD))

def reference(tokens, segment, first_norm_scale, first_norm_bias, w_qkv, q_bias, v_bias, w_o, o_bias, second_norm_scale, second_norm_bias, w_fc, fc_bias, w_pr, pr_bias, cotangent):
    w_flat = w_qkv.reshape(D, 3 * D)

    def one_block(totals, inputs_block):
        tok_blk, seg_blk, block_cotangents = inputs_block
        token_floats = tok_blk.astype(jnp.float32)
        first_normalized, first_inverse_deviation = apply_layer_norm(token_floats)
        first_normed = (first_normalized * first_norm_scale + first_norm_bias).astype(jnp.bfloat16)
        proj = jnp.dot(first_normed, w_flat, preferred_element_type=jnp.float32).reshape(CAP, 3, D)
        queries = (proj[:, 0] + q_bias).astype(jnp.bfloat16)
        keys_in = proj[:, 1].astype(jnp.bfloat16)
        vals_in = (proj[:, 2] + v_bias).astype(jnp.bfloat16)
        att, lse = attend(queries, keys_in, vals_in, seg_blk)
        residual_stream = token_floats + jnp.dot(att, w_o, preferred_element_type=jnp.float32) + o_bias
        second_normalized, second_inverse_deviation = apply_layer_norm(residual_stream)
        second_normed = (second_normalized * second_norm_scale + second_norm_bias).astype(jnp.bfloat16)
        pre_act = jnp.dot(second_normed, w_fc, preferred_element_type=jnp.float32) + fc_bias
        act = gelu_value(pre_act).astype(jnp.bfloat16)
        out_blk = (residual_stream + (jnp.dot(act, w_pr, preferred_element_type=jnp.float32) + pr_bias)).astype(jnp.bfloat16)
        gw_pr = jnp.dot(act.T, block_cotangents, preferred_element_type=jnp.float32)
        gb_pr = lax.optimization_barrier(jnp.sum(block_cotangents.astype(jnp.float32), axis=0))
        grad_pre = jnp.dot(block_cotangents, w_pr.T, preferred_element_type=jnp.float32) * gelu_slope(pre_act)
        grad_pre_b = grad_pre.astype(jnp.bfloat16)
        gw_fc = jnp.dot(second_normed.T, grad_pre_b, preferred_element_type=jnp.float32)
        gb_fc = lax.optimization_barrier(jnp.sum(grad_pre, axis=0))
        second_normed_gradient = jnp.dot(grad_pre_b, w_fc.T, preferred_element_type=jnp.float32)
        second_gain_gradient = lax.optimization_barrier(jnp.sum(second_normed_gradient * second_normalized, axis=0))
        gbb_two = lax.optimization_barrier(jnp.sum(second_normed_gradient, axis=0))
        residual_gradient = block_cotangents.astype(jnp.float32) + norm_gradient(second_normed_gradient * second_norm_scale, second_normalized, second_inverse_deviation)
        grad_resid_b = residual_gradient.astype(jnp.bfloat16)
        gw_o = jnp.dot(att.T, grad_resid_b, preferred_element_type=jnp.float32)
        gb_o = lax.optimization_barrier(jnp.sum(residual_gradient, axis=0))
        grad_att = jnp.dot(grad_resid_b, w_o.T, preferred_element_type=jnp.float32).astype(jnp.bfloat16)
        grad_q, grad_k, grad_v = attend_back(queries, keys_in, vals_in, att, grad_att, lse, seg_blk)
        gq_bias = lax.optimization_barrier(jnp.sum(grad_q, axis=0))
        gv_bias = lax.optimization_barrier(jnp.sum(grad_v, axis=0))
        grad_qkv = jnp.stack([grad_q, grad_k, grad_v], axis=1).astype(jnp.bfloat16).reshape(CAP, 3 * D)
        gw_qkv = jnp.dot(first_normed.T, grad_qkv, preferred_element_type=jnp.float32).reshape(D, 3, D)
        first_normed_gradient = jnp.dot(grad_qkv, w_flat.T, preferred_element_type=jnp.float32)
        first_gain_gradient = lax.optimization_barrier(jnp.sum(first_normed_gradient * first_normalized, axis=0))
        gbb_one = lax.optimization_barrier(jnp.sum(first_normed_gradient, axis=0))
        token_gradient = residual_gradient + norm_gradient(first_normed_gradient * first_norm_scale, first_normalized, first_inverse_deviation)
        terms = (first_gain_gradient, gbb_one, gw_qkv, gq_bias, gv_bias, gw_o, gb_o, second_gain_gradient, gbb_two, gw_fc, gb_fc, gw_pr, gb_pr)
        return (jax.tree.map(lambda left, right: left + right, totals, terms), (out_blk, token_gradient))
    zeros_init = (jnp.zeros((D,), jnp.float32), jnp.zeros((D,), jnp.float32), jnp.zeros((D, 3, D), jnp.float32), jnp.zeros((D,), jnp.float32), jnp.zeros((D,), jnp.float32), jnp.zeros((D, D), jnp.float32), jnp.zeros((D,), jnp.float32), jnp.zeros((D,), jnp.float32), jnp.zeros((D,), jnp.float32), jnp.zeros((D, FF), jnp.float32), jnp.zeros((FF,), jnp.float32), jnp.zeros((FF, D), jnp.float32), jnp.zeros((D,), jnp.float32))
    totals, (outs_all, grads_tok) = lax.scan(one_block, zeros_init, (tokens.reshape(N_DP, CAP, D), segment.reshape(N_DP, CAP), cotangent.reshape(N_DP, CAP, D)))
    return (outs_all.reshape(TOKENS, D), grads_tok.reshape(TOKENS, D), totals[0], totals[1], totals[2], totals[3], totals[4], totals[5], totals[6], totals[7], totals[8], totals[9], totals[10], totals[11], totals[12])
```

```python
import math

import jax
import jax.numpy as jnp
from jax import lax
from jax.sharding import PartitionSpec as P

HEAD = 64


gelu_cubic = 0.044715
root_two_pi = math.sqrt(2.0 / math.pi)


def apply_layer_norm(residual_stream):
    center = residual_stream - jnp.mean(residual_stream, axis=-1, keepdims=True)
    inverse_deviation = lax.rsqrt(jnp.mean(center * center, axis=-1, keepdims=True) + 1e-05)
    return (center * inverse_deviation, inverse_deviation)


def norm_gradient(centered_gradient, normalized_input, inverse_deviation):
    return inverse_deviation * (
        centered_gradient
        - jnp.mean(centered_gradient, axis=-1, keepdims=True)
        - normalized_input * jnp.mean(centered_gradient * normalized_input, axis=-1, keepdims=True)
    )


def gelu_value(pre):
    inner = root_two_pi * (pre + gelu_cubic * pre * pre * pre)
    return 0.5 * pre * (1.0 + jnp.tanh(inner))


def gelu_slope(pre):
    tanh_val = jnp.tanh(root_two_pi * (pre + gelu_cubic * pre * pre * pre))
    return 0.5 * (1.0 + tanh_val) + 0.5 * pre * (1.0 - tanh_val * tanh_val) * root_two_pi * (
        1.0 + 3.0 * gelu_cubic * pre * pre
    )


def allowed_pairs(segment, block_rows):
    query_pos = jnp.arange(block_rows)
    key_pos = jnp.arange(segment.shape[0])
    same = segment[:, None] == segment[None, :]
    return same & (key_pos[None, :] <= query_pos[:, None])


def score_block(query_blk, key_heads, allowed, score_scale):
    scores = (
        jnp.einsum("qhe,khe->hqk", query_blk, key_heads, preferred_element_type=jnp.float32)
        * score_scale
    )
    return jnp.where(allowed[None], scores, -1e30)


def attend(queries, keys_in, vals_in, segment):
    rows_all = queries.shape[0]
    local_heads = queries.shape[1] // HEAD
    query_h = queries.reshape(rows_all, local_heads, HEAD)
    key_h = keys_in.reshape(rows_all, local_heads, HEAD)
    val_h = vals_in.reshape(rows_all, local_heads, HEAD)
    block_rows = min(512, rows_all)
    score_scale = 1.0 / math.sqrt(HEAD)
    allowed = allowed_pairs(segment, block_rows)
    scores = score_block(query_h, key_h, allowed, score_scale)
    row_max = jnp.max(scores, axis=-1, keepdims=True)
    raw = jnp.exp(scores - row_max)
    row_total = jnp.sum(raw, axis=-1, keepdims=True)
    probs = (raw / row_total).astype(jnp.bfloat16)
    mixed_part = jnp.einsum(
        "hqk,khe->qhe", probs, val_h, preferred_element_type=jnp.float32
    ).astype(jnp.bfloat16)
    outputs = mixed_part.reshape(block_rows, local_heads * HEAD)
    totals = (row_max + jnp.log(row_total))[..., 0]
    return (outputs, totals)


def attend_back(queries, keys_in, vals_in, att, grad_att, lse, segment):
    rows_all = queries.shape[0]
    local_heads = queries.shape[1] // HEAD
    query_h = queries.reshape(rows_all, local_heads, HEAD)
    key_h = keys_in.reshape(rows_all, local_heads, HEAD)
    val_h = vals_in.reshape(rows_all, local_heads, HEAD)
    att_h = att.reshape(rows_all, local_heads, HEAD)
    grad_h = grad_att.reshape(rows_all, local_heads, HEAD)
    block_rows = min(512, rows_all)
    score_scale = 1.0 / math.sqrt(HEAD)
    allowed = allowed_pairs(segment, block_rows)
    scores = score_block(query_h, key_h, allowed, score_scale)
    probs_f = jnp.exp(scores - lse[:, 0:block_rows, None])
    probs_b = probs_f.astype(jnp.bfloat16)
    grad_val_sum = jnp.einsum("hqk,qhe->khe", probs_b, grad_h, preferred_element_type=jnp.float32)
    dprob = jnp.einsum("qhe,khe->hqk", grad_h, val_h, preferred_element_type=jnp.float32)
    delta = jnp.sum(grad_h.astype(jnp.float32) * att_h.astype(jnp.float32), axis=-1).T
    grad_score = (probs_f * (dprob - delta[:, :, None])).astype(jnp.bfloat16)
    query_parts = (
        jnp.einsum("hqk,khe->qhe", grad_score, key_h, preferred_element_type=jnp.float32)
        * score_scale
    ).reshape(block_rows, local_heads * HEAD)
    grad_key_sum = (
        jnp.einsum("hqk,qhe->khe", grad_score, query_h, preferred_element_type=jnp.float32)
        * score_scale
    )
    return (
        query_parts,
        grad_key_sum.reshape(rows_all, local_heads * HEAD),
        grad_val_sum.reshape(rows_all, local_heads * HEAD),
    )


def swap_sum(part, size):
    sent = part.astype(jnp.bfloat16)
    total = part
    for shift in range(1, size):
        pairs = [(i, (i + shift) % size) for i in range(size)]
        total = total + lax.ppermute(sent, "tensor", pairs).astype(jnp.float32)
    return total


def swap_scatter(part, size, width):
    me = lax.axis_index("tensor")
    total = lax.dynamic_slice_in_dim(part, me * width, width, 1).astype(jnp.float32)
    for shift in range(1, size):
        pairs = [(i, (i + shift) % size) for i in range(size)]
        target = lax.rem(me + shift, size)
        sent = lax.dynamic_slice_in_dim(part, target * width, width, 1).astype(jnp.bfloat16)
        total = total + lax.ppermute(sent, "tensor", pairs).astype(jnp.float32)
    return total


def swap_gather(own, size):
    if size != 2:
        return lax.all_gather(own, "tensor", axis=1, tiled=True)
    other = lax.ppermute(own, "tensor", [(0, 1), (1, 0)])
    first = lax.axis_index("tensor") == 0
    return jnp.concatenate(
        [jnp.where(first, own, other), jnp.where(first, other, own)], axis=1
    )


def halving(part, groups, order, wire):
    me = lax.axis_index("dp")
    rows, columns = part.shape[1:]
    bits = []
    size = groups
    while size > 1:
        bits.append(len(bits))
        size //= 2
    sequence = [bit for bit in order if bit in bits]
    sequence += [bit for bit in bits if bit not in sequence]
    left = list(reversed(bits))
    current = part
    for step, bit in enumerate(sequence):
        place = left.index(bit)
        high, low = 2**place, 2 ** (len(left) - place - 1)
        grid = current.reshape(high, 2, low, rows, columns)
        mine = (me >> bit) & 1
        keep = lax.dynamic_index_in_dim(grid, mine, 1, keepdims=False)
        send = lax.dynamic_index_in_dim(grid, 1 - mine, 1, keepdims=False).astype(wire)
        got = lax.ppermute(send, "dp", [(i, i ^ (1 << bit)) for i in range(groups)])
        current = keep.astype(jnp.float32) + got.astype(jnp.float32)
        if step < len(sequence) - 1:
            current = current.astype(wire)
        left.remove(bit)
    return current.reshape(rows, columns)


X_FIRST, Y_FIRST, Z_FIRST = (0, 1, 2, 3), (1, 0, 2, 3), (2, 0, 1, 3)


def body(
    tokens,
    segment,
    first_norm_scale,
    first_norm_bias,
    w_qkv,
    q_bias,
    v_bias,
    w_o,
    o_bias,
    second_norm_scale,
    second_norm_bias,
    w_fc,
    fc_bias,
    w_pr,
    pr_bias,
    cotangent,
):
    rows_here = tokens.shape[0]
    shard_width = tokens.shape[1]
    total_width = w_qkv.shape[0]
    groups = lax.axis_size("dp")
    cores = lax.axis_size("tensor")
    column_offset = lax.axis_index("tensor") * shard_width
    tok_full = swap_gather(tokens, cores)
    complete_cotangents = swap_gather(cotangent, cores)
    token_floats = tok_full.astype(jnp.float32)
    first_normalized, first_inverse_deviation = apply_layer_norm(token_floats)
    first_normed = (first_normalized * first_norm_scale + first_norm_bias).astype(jnp.bfloat16)
    w_flat = w_qkv.reshape(total_width, 3 * shard_width)
    proj = jnp.dot(first_normed, w_flat, preferred_element_type=jnp.float32).reshape(
        rows_here, 3, shard_width
    )
    queries = (proj[:, 0] + q_bias).astype(jnp.bfloat16)
    keys_in = proj[:, 1].astype(jnp.bfloat16)
    vals_in = (proj[:, 2] + v_bias).astype(jnp.bfloat16)
    att, lse = attend(queries, keys_in, vals_in, segment)
    partial_out = jnp.dot(att, w_o, preferred_element_type=jnp.float32)
    residual_stream = token_floats + swap_sum(partial_out, cores) + o_bias
    second_normalized, second_inverse_deviation = apply_layer_norm(residual_stream)
    second_normed = (second_normalized * second_norm_scale + second_norm_bias).astype(jnp.bfloat16)
    pre_act = jnp.dot(second_normed, w_fc, preferred_element_type=jnp.float32) + fc_bias
    act = gelu_value(pre_act).astype(jnp.bfloat16)
    mlp_part = swap_scatter(
        jnp.dot(act, w_pr, preferred_element_type=jnp.float32), cores, shard_width
    )
    resid_own = lax.dynamic_slice_in_dim(residual_stream, column_offset, shard_width, 1)
    block_out = (
        resid_own + (mlp_part + lax.dynamic_slice_in_dim(pr_bias, column_offset, shard_width, 0))
    ).astype(jnp.bfloat16)
    gw_pr = jnp.dot(act.T, complete_cotangents, preferred_element_type=jnp.float32)
    pr_blocks = gw_pr.astype(jnp.bfloat16).reshape(groups, -1, total_width)
    pr_half = pr_blocks.shape[1] // 2
    own_pr = jnp.concatenate(
        [
            halving(pr_blocks[:, :pr_half], groups, X_FIRST, jnp.bfloat16),
            halving(pr_blocks[:, pr_half:], groups, Y_FIRST, jnp.bfloat16),
        ],
        axis=0,
    )
    gb_pr = jnp.sum(complete_cotangents.astype(jnp.float32), axis=0)
    grad_pre = jnp.dot(
        complete_cotangents, w_pr.T, preferred_element_type=jnp.float32
    ) * gelu_slope(pre_act)
    grad_pre_b = grad_pre.astype(jnp.bfloat16)
    gw_fc = jnp.dot(second_normed.T, grad_pre_b, preferred_element_type=jnp.float32)
    fc_blocks = gw_fc.astype(jnp.bfloat16).reshape(groups, total_width // groups, -1)
    fc_half = fc_blocks.shape[2] // 2
    own_fc = jnp.concatenate(
        [
            halving(fc_blocks[:, :, :fc_half], groups, X_FIRST, jnp.bfloat16),
            halving(fc_blocks[:, :, fc_half:], groups, Y_FIRST, jnp.bfloat16),
        ],
        axis=1,
    )
    gb_fc = jnp.sum(grad_pre, axis=0)
    partial_h2 = jnp.dot(grad_pre_b, w_fc.T, preferred_element_type=jnp.float32)
    second_normed_gradient = swap_sum(partial_h2, cores)
    second_gain_gradient = jnp.sum(second_normed_gradient * second_normalized, axis=0)
    gbb_two = jnp.sum(second_normed_gradient, axis=0)
    residual_gradient = complete_cotangents.astype(jnp.float32) + norm_gradient(
        second_normed_gradient * second_norm_scale, second_normalized, second_inverse_deviation
    )
    grad_resid_b = residual_gradient.astype(jnp.bfloat16)
    gw_o = jnp.dot(att.T, grad_resid_b, preferred_element_type=jnp.float32)
    own_o = halving(
        gw_o.astype(jnp.bfloat16).reshape(groups, -1, total_width), groups, X_FIRST, jnp.bfloat16
    )
    gb_o = jnp.sum(residual_gradient, axis=0)
    grad_att = jnp.dot(grad_resid_b, w_o.T, preferred_element_type=jnp.float32).astype(jnp.bfloat16)
    grad_q, grad_k, grad_v = attend_back(queries, keys_in, vals_in, att, grad_att, lse, segment)
    gq_bias = jnp.sum(grad_q, axis=0)
    gv_bias = jnp.sum(grad_v, axis=0)
    grad_parts = [part.astype(jnp.bfloat16) for part in (grad_q, grad_k, grad_v)]
    grad_qkv = jnp.concatenate(grad_parts, axis=1)
    own_qkv = jnp.stack(
        [
            halving(
                jnp.dot(first_normed.T, part, preferred_element_type=jnp.float32)
                .astype(jnp.bfloat16)
                .reshape(groups, total_width // groups, shard_width),
                groups,
                order,
                jnp.bfloat16,
            )
            for part, order in zip(grad_parts, (X_FIRST, Y_FIRST, Z_FIRST))
        ],
        axis=1,
    )
    first_normed_gradient = swap_scatter(
        jnp.dot(grad_qkv, w_flat.T, preferred_element_type=jnp.float32), cores, shard_width
    )
    owned_normalized = lax.dynamic_slice_in_dim(first_normalized, column_offset, shard_width, 1)
    centered_gradient = first_normed_gradient * lax.dynamic_slice_in_dim(
        first_norm_scale, column_offset, shard_width, 0
    )
    row_sums = jnp.stack(
        [jnp.sum(centered_gradient, axis=1), jnp.sum(centered_gradient * owned_normalized, axis=1)]
    )
    all_sums = row_sums
    for shift in range(1, cores):
        pairs = [(i, (i + shift) % cores) for i in range(cores)]
        all_sums = all_sums + lax.ppermute(row_sums, "tensor", pairs)
    gradient_sum, weighted_gradient_sum = all_sums[0], all_sums[1]
    grad_own = lax.dynamic_slice_in_dim(residual_gradient, column_offset, shard_width, 1)
    grad_tokens = grad_own + first_inverse_deviation * (
        centered_gradient
        - gradient_sum[:, None] / total_width
        - owned_normalized * (weighted_gradient_sum[:, None] / total_width)
    )
    first_gain_gradient = jnp.sum(first_normed_gradient * owned_normalized, axis=0)
    gbb_one = jnp.sum(first_normed_gradient, axis=0)
    vectors = (
        first_gain_gradient,
        gbb_one,
        gq_bias,
        gv_bias,
        gb_o,
        second_gain_gradient,
        gbb_two,
        gb_fc,
        gb_pr,
    )
    packed = jnp.concatenate([piece.reshape(groups, 1, -1) for piece in vectors], axis=2)
    own_vectors = halving(packed, groups, Y_FIRST, jnp.float32)[0]
    pieces = []
    offset = 0
    for piece in vectors:
        length = piece.shape[0] // groups
        pieces.append(own_vectors[offset : offset + length])
        offset += length
    gain_one, bias_one, q_own, v_own, o_own, gain_two, bias_two, fc_own, pr_own = pieces
    return (
        block_out,
        grad_tokens,
        gain_one,
        bias_one,
        own_qkv,
        q_own,
        v_own,
        own_o,
        o_own,
        gain_two,
        bias_two,
        own_fc,
        fc_own,
        own_pr,
        pr_own,
    )


def solution(mesh):
    placed = (
        P("dp", "tensor"),
        P("dp"),
        P(),
        P(),
        P(None, None, "tensor"),
        P("tensor"),
        P("tensor"),
        P("tensor", None),
        P(),
        P(),
        P(),
        P(None, "tensor"),
        P("tensor"),
        P("tensor", None),
        P(),
        P("dp", "tensor"),
    )
    return jax.shard_map(
        body,
        mesh=mesh,
        in_specs=placed,
        out_specs=(
            P("dp", "tensor"),
            P("dp", "tensor"),
            P(("tensor", "dp")),
            P(("tensor", "dp")),
            P("dp", None, "tensor"),
            P(("tensor", "dp")),
            P(("tensor", "dp")),
            P(("tensor", "dp"), None),
            P("dp"),
            P("dp"),
            P("dp"),
            P("dp", "tensor"),
            P(("tensor", "dp")),
            P(("tensor", "dp"), None),
            P("dp"),
        ),
        check_vma=False,
    )
```

```python
import functools
import heapq
import math

import jax
import jax.numpy as jnp
from jax import lax
from jax.experimental import pallas as pl
from jax.experimental.pallas import tpu as pltpu
from jax.sharding import PartitionSpec as P

HEAD = 64


gelu_cubic = 0.044715
root_two_pi = math.sqrt(2.0 / math.pi)


def apply_layer_norm(residual_stream):
    center = residual_stream - jnp.mean(residual_stream, axis=-1, keepdims=True)
    inverse_deviation = lax.rsqrt(jnp.mean(center * center, axis=-1, keepdims=True) + 1e-05)
    return (center * inverse_deviation, inverse_deviation)


def norm_gradient(centered_gradient, normalized_input, inverse_deviation):
    return inverse_deviation * (
        centered_gradient
        - jnp.mean(centered_gradient, axis=-1, keepdims=True)
        - normalized_input * jnp.mean(centered_gradient * normalized_input, axis=-1, keepdims=True)
    )


def gelu_value(pre):
    inner = root_two_pi * (pre + gelu_cubic * pre * pre * pre)
    return 0.5 * pre * (1.0 + jnp.tanh(inner))


def gelu_slope(pre):
    tanh_val = jnp.tanh(root_two_pi * (pre + gelu_cubic * pre * pre * pre))
    return 0.5 * (1.0 + tanh_val) + 0.5 * pre * (1.0 - tanh_val * tanh_val) * root_two_pi * (
        1.0 + 3.0 * gelu_cubic * pre * pre
    )


def allowed_pairs(segment, block_rows):
    query_pos = jnp.arange(block_rows)
    key_pos = jnp.arange(segment.shape[0])
    same = segment[:, None] == segment[None, :]
    return same & (key_pos[None, :] <= query_pos[:, None])


def score_block(query_blk, key_heads, allowed, score_scale):
    scores = (
        jnp.einsum("qhe,khe->hqk", query_blk, key_heads, preferred_element_type=jnp.float32)
        * score_scale
    )
    return jnp.where(allowed[None], scores, -1e30)


def attend(queries, keys_in, vals_in, segment):
    rows_all = queries.shape[0]
    local_heads = queries.shape[1] // HEAD
    query_h = queries.reshape(rows_all, local_heads, HEAD)
    key_h = keys_in.reshape(rows_all, local_heads, HEAD)
    val_h = vals_in.reshape(rows_all, local_heads, HEAD)
    block_rows = min(512, rows_all)
    score_scale = 1.0 / math.sqrt(HEAD)
    allowed = allowed_pairs(segment, block_rows)
    scores = score_block(query_h, key_h, allowed, score_scale)
    row_max = jnp.max(scores, axis=-1, keepdims=True)
    raw = jnp.exp(scores - row_max)
    row_total = jnp.sum(raw, axis=-1, keepdims=True)
    probs = (raw / row_total).astype(jnp.bfloat16)
    mixed_part = jnp.einsum(
        "hqk,khe->qhe", probs, val_h, preferred_element_type=jnp.float32
    ).astype(jnp.bfloat16)
    outputs = mixed_part.reshape(block_rows, local_heads * HEAD)
    totals = (row_max + jnp.log(row_total))[..., 0]
    return (outputs, totals)


def attend_back(queries, keys_in, vals_in, att, grad_att, lse, segment):
    rows_all = queries.shape[0]
    local_heads = queries.shape[1] // HEAD
    query_h = queries.reshape(rows_all, local_heads, HEAD)
    key_h = keys_in.reshape(rows_all, local_heads, HEAD)
    val_h = vals_in.reshape(rows_all, local_heads, HEAD)
    att_h = att.reshape(rows_all, local_heads, HEAD)
    grad_h = grad_att.reshape(rows_all, local_heads, HEAD)
    block_rows = min(512, rows_all)
    score_scale = 1.0 / math.sqrt(HEAD)
    allowed = allowed_pairs(segment, block_rows)
    scores = score_block(query_h, key_h, allowed, score_scale)
    probs_f = jnp.exp(scores - lse[:, 0:block_rows, None])
    probs_b = probs_f.astype(jnp.bfloat16)
    grad_val_sum = jnp.einsum("hqk,qhe->khe", probs_b, grad_h, preferred_element_type=jnp.float32)
    dprob = jnp.einsum("qhe,khe->hqk", grad_h, val_h, preferred_element_type=jnp.float32)
    delta = jnp.sum(grad_h.astype(jnp.float32) * att_h.astype(jnp.float32), axis=-1).T
    grad_score = (probs_f * (dprob - delta[:, :, None])).astype(jnp.bfloat16)
    query_parts = (
        jnp.einsum("hqk,khe->qhe", grad_score, key_h, preferred_element_type=jnp.float32)
        * score_scale
    ).reshape(block_rows, local_heads * HEAD)
    grad_key_sum = (
        jnp.einsum("hqk,qhe->khe", grad_score, query_h, preferred_element_type=jnp.float32)
        * score_scale
    )
    return (
        query_parts,
        grad_key_sum.reshape(rows_all, local_heads * HEAD),
        grad_val_sum.reshape(rows_all, local_heads * HEAD),
    )


def swap_sum(part, size):
    sent = part.astype(jnp.bfloat16)
    total = part
    for shift in range(1, size):
        pairs = [(i, (i + shift) % size) for i in range(size)]
        total = total + lax.ppermute(sent, "tensor", pairs).astype(jnp.float32)
    return total


def swap_scatter(part, size, width):
    me = lax.axis_index("tensor")
    total = lax.dynamic_slice_in_dim(part, me * width, width, 1).astype(jnp.float32)
    for shift in range(1, size):
        pairs = [(i, (i + shift) % size) for i in range(size)]
        target = lax.rem(me + shift, size)
        sent = lax.dynamic_slice_in_dim(part, target * width, width, 1).astype(jnp.bfloat16)
        total = total + lax.ppermute(sent, "tensor", pairs).astype(jnp.float32)
    return total


def swap_gather(own, size):
    if size != 2:
        return lax.all_gather(own, "tensor", axis=1, tiled=True)
    other = lax.ppermute(own, "tensor", [(0, 1), (1, 0)])
    first = lax.axis_index("tensor") == 0
    return jnp.concatenate(
        [jnp.where(first, own, other), jnp.where(first, other, own)], axis=1
    )


def bits_of(groups):
    return list(range(groups.bit_length() - 1))


def split_blocks(part, groups, order):
    bits = bits_of(groups)
    sequence = [bit for bit in order if bit in bits]
    sequence += [bit for bit in bits if bit not in sequence]
    left = bits[::-1]
    return part.reshape((2,) * len(left) + part.shape[1:]), left, sequence


def first_step(chunk, groups):
    current, left, sequence = chunk
    bit = sequence[0]
    me = lax.axis_index("dp")
    mine = (me >> bit) & 1
    place = left.index(bit)
    keep = lax.dynamic_index_in_dim(current, mine, place, keepdims=False)
    send = lax.dynamic_index_in_dim(current, 1 - mine, place, keepdims=False)
    got = lax.ppermute(send, "dp", [(i, i ^ (1 << bit)) for i in range(groups)])
    total = (keep.astype(jnp.float32) + got.astype(jnp.float32)).astype(current.dtype)
    return total, [b for b in left if b != bit], sequence[1:]


def arrival_order(chunks):
    free = {}
    queue = []

    def issue(now, index, step):
        array, left, sequence = chunks[index]
        bit = sequence[step]
        link = min(bit, 2)
        size = array.size * array.dtype.itemsize / 2 ** (step + 1)
        start = max(now, free.get(link, 0.0))
        end = start + size / 46e3 * (2 if bit > 2 else 1)
        free[link] = end
        heapq.heappush(queue, (end + 2.0, index, step))

    for index in range(len(chunks)):
        issue(0.0, index, 0)
    result = []
    while queue:
        now, index, step = heapq.heappop(queue)
        result.append((index, step))
        if step + 1 < len(chunks[index][2]):
            issue(now + 0.3, index, step + 1)
    return result


def reduce_kernel(meta, events, *refs):
    count = len(meta)
    sources = refs[:count]
    results = refs[count : 2 * count]
    landing = []
    position = 2 * count
    for left, sequence in meta:
        landing.append(refs[position : position + len(sequence)])
        position += len(sequence)
    send_sem, recv_sem = refs[position], refs[position + 1]
    me = lax.axis_index("dp")
    used = sorted({bit for _, sequence in meta for bit in sequence})

    def mine_of(bit):
        return lax.rem(me // (1 << bit), 2)

    def partner(bit):
        return me + (1 - 2 * mine_of(bit)) * (1 << bit)

    barrier = pltpu.get_barrier_semaphore()
    for bit in used:
        pl.semaphore_signal(
            barrier, inc=1, device_id={"dp": partner(bit)}, device_id_type=pl.DeviceIdType.MESH
        )
    pl.semaphore_wait(barrier, len(used))

    def left_at(index, step):
        left, sequence = meta[index]
        return [bit for bit in left if bit not in sequence[:step]]

    def held(index, step):
        return sources[index] if step == 0 else landing[index][step - 1]

    def copy_of(index, step):
        bit = meta[index][1][step]
        place = left_at(index, step).index(bit)
        lead = (slice(None),) * place + (1 - mine_of(bit),)
        return pltpu.make_async_remote_copy(
            src_ref=held(index, step).at[lead],
            dst_ref=landing[index][step],
            send_sem=send_sem.at[index, step],
            recv_sem=recv_sem.at[index, step],
            device_id={"dp": partner(bit)},
            device_id_type=pl.DeviceIdType.MESH,
        )

    for index in range(count):
        copy_of(index, 0).start()
    for index, step in events:
        copy_of(index, step).wait_recv()
        left, sequence = meta[index]
        bit = sequence[step]
        before = left_at(index, step)
        place = before.index(bit)
        source, target = held(index, step), landing[index][step]
        last = step == len(sequence) - 1
        for flat in range(2 ** (len(before) - 1)):
            rest = [(flat >> k) & 1 for k in range(len(before) - 1)]
            full = tuple(rest[:place]) + (mine_of(bit),) + tuple(rest[place:])
            total = source[full].astype(jnp.float32) + target[tuple(rest)].astype(jnp.float32)
            if last:
                results[index][...] = total
            else:
                target[tuple(rest)] = total.astype(target.dtype)
        if not last:
            copy_of(index, step + 1).start()
    for index, (left, sequence) in enumerate(meta):
        for step in range(len(sequence)):
            copy_of(index, step).wait_send()


def reduce_blocks(chunks):
    meta = [(left, sequence) for _, left, sequence in chunks]
    arrays = [array for array, _, _ in chunks]
    scratch = []
    for array, left, sequence in chunks:
        tail = array.shape[len(left) :]
        for step in range(len(sequence)):
            scratch.append(pltpu.VMEM((2,) * (len(left) - step - 1) + tail, array.dtype))
    steps = max(len(sequence) for _, sequence in meta)
    sems = pltpu.SemaphoreType.DMA((len(chunks), steps))
    return pl.pallas_call(
        functools.partial(reduce_kernel, meta, arrival_order(chunks)),
        out_shape=[
            jax.ShapeDtypeStruct(array.shape[len(left) :], jnp.float32)
            for array, left, _ in chunks
        ],
        in_specs=[pl.BlockSpec(memory_space=pltpu.VMEM)] * len(arrays),
        out_specs=[pl.BlockSpec(memory_space=pltpu.VMEM)] * len(arrays),
        scratch_shapes=scratch + [sems, sems],
        compiler_params=pltpu.CompilerParams(
            collective_id=0, has_side_effects=True, vmem_limit_bytes=48 << 20
        ),
    )(*arrays)


X_FIRST, Y_FIRST, Z_FIRST = (0, 1, 2, 3), (1, 0, 2, 3), (2, 0, 1, 3)


def body(
    tokens,
    segment,
    first_norm_scale,
    first_norm_bias,
    w_qkv,
    q_bias,
    v_bias,
    w_o,
    o_bias,
    second_norm_scale,
    second_norm_bias,
    w_fc,
    fc_bias,
    w_pr,
    pr_bias,
    cotangent,
):
    rows_here = tokens.shape[0]
    shard_width = tokens.shape[1]
    total_width = w_qkv.shape[0]
    groups = lax.axis_size("dp")
    cores = lax.axis_size("tensor")
    column_offset = lax.axis_index("tensor") * shard_width
    tok_full = swap_gather(tokens, cores)
    complete_cotangents = swap_gather(cotangent, cores)
    token_floats = tok_full.astype(jnp.float32)
    first_normalized, first_inverse_deviation = apply_layer_norm(token_floats)
    first_normed = (first_normalized * first_norm_scale + first_norm_bias).astype(jnp.bfloat16)
    w_flat = w_qkv.reshape(total_width, 3 * shard_width)
    proj = jnp.dot(first_normed, w_flat, preferred_element_type=jnp.float32).reshape(
        rows_here, 3, shard_width
    )
    queries = (proj[:, 0] + q_bias).astype(jnp.bfloat16)
    keys_in = proj[:, 1].astype(jnp.bfloat16)
    vals_in = (proj[:, 2] + v_bias).astype(jnp.bfloat16)
    att, lse = attend(queries, keys_in, vals_in, segment)
    partial_out = jnp.dot(att, w_o, preferred_element_type=jnp.float32)
    residual_stream = token_floats + swap_sum(partial_out, cores) + o_bias
    second_normalized, second_inverse_deviation = apply_layer_norm(residual_stream)
    second_normed = (second_normalized * second_norm_scale + second_norm_bias).astype(jnp.bfloat16)
    pre_act = jnp.dot(second_normed, w_fc, preferred_element_type=jnp.float32) + fc_bias
    act = gelu_value(pre_act).astype(jnp.bfloat16)
    mlp_part = swap_scatter(
        jnp.dot(act, w_pr, preferred_element_type=jnp.float32), cores, shard_width
    )
    resid_own = lax.dynamic_slice_in_dim(residual_stream, column_offset, shard_width, 1)
    block_out = (
        resid_own + (mlp_part + lax.dynamic_slice_in_dim(pr_bias, column_offset, shard_width, 0))
    ).astype(jnp.bfloat16)
    gw_pr = jnp.dot(act.T, complete_cotangents, preferred_element_type=jnp.float32)
    pr_blocks = gw_pr.astype(jnp.bfloat16).reshape(groups, -1, total_width)
    pr_half = pr_blocks.shape[1] // 2
    pr_chunks = [
        first_step(split_blocks(pr_blocks[:, :pr_half], groups, X_FIRST), groups),
        first_step(split_blocks(pr_blocks[:, pr_half:], groups, Y_FIRST), groups),
    ]
    gb_pr = jnp.sum(complete_cotangents.astype(jnp.float32), axis=0)
    grad_pre = jnp.dot(
        complete_cotangents, w_pr.T, preferred_element_type=jnp.float32
    ) * gelu_slope(pre_act)
    grad_pre_b = grad_pre.astype(jnp.bfloat16)
    gw_fc = jnp.dot(second_normed.T, grad_pre_b, preferred_element_type=jnp.float32)
    fc_blocks = gw_fc.astype(jnp.bfloat16).reshape(groups, total_width // groups, -1)
    fc_half = fc_blocks.shape[2] // 2
    fc_chunks = [
        first_step(split_blocks(fc_blocks[:, :, :fc_half], groups, X_FIRST), groups),
        first_step(split_blocks(fc_blocks[:, :, fc_half:], groups, Y_FIRST), groups),
    ]
    gb_fc = jnp.sum(grad_pre, axis=0)
    partial_h2 = jnp.dot(grad_pre_b, w_fc.T, preferred_element_type=jnp.float32)
    second_normed_gradient = swap_sum(partial_h2, cores)
    second_gain_gradient = jnp.sum(second_normed_gradient * second_normalized, axis=0)
    gbb_two = jnp.sum(second_normed_gradient, axis=0)
    residual_gradient = complete_cotangents.astype(jnp.float32) + norm_gradient(
        second_normed_gradient * second_norm_scale, second_normalized, second_inverse_deviation
    )
    grad_resid_b = residual_gradient.astype(jnp.bfloat16)
    gw_o = jnp.dot(att.T, grad_resid_b, preferred_element_type=jnp.float32)
    o_chunk = split_blocks(
        gw_o.astype(jnp.bfloat16).reshape(groups, -1, total_width), groups, Z_FIRST
    )
    gb_o = jnp.sum(residual_gradient, axis=0)
    grad_att = jnp.dot(grad_resid_b, w_o.T, preferred_element_type=jnp.float32).astype(jnp.bfloat16)
    grad_q, grad_k, grad_v = attend_back(queries, keys_in, vals_in, att, grad_att, lse, segment)
    gq_bias = jnp.sum(grad_q, axis=0)
    gv_bias = jnp.sum(grad_v, axis=0)
    grad_parts = [part.astype(jnp.bfloat16) for part in (grad_q, grad_k, grad_v)]
    grad_qkv = jnp.concatenate(grad_parts, axis=1)
    qkv_chunks = [
        split_blocks(
            jnp.dot(first_normed.T, part, preferred_element_type=jnp.float32)
            .astype(jnp.bfloat16)
            .reshape(groups, total_width // groups, shard_width),
            groups,
            order,
        )
        for part, order in zip(grad_parts, (X_FIRST, Y_FIRST, Z_FIRST))
    ]
    first_normed_gradient = swap_scatter(
        jnp.dot(grad_qkv, w_flat.T, preferred_element_type=jnp.float32), cores, shard_width
    )
    owned_normalized = lax.dynamic_slice_in_dim(first_normalized, column_offset, shard_width, 1)
    centered_gradient = first_normed_gradient * lax.dynamic_slice_in_dim(
        first_norm_scale, column_offset, shard_width, 0
    )
    row_sums = jnp.stack(
        [jnp.sum(centered_gradient, axis=1), jnp.sum(centered_gradient * owned_normalized, axis=1)]
    )
    all_sums = row_sums
    for shift in range(1, cores):
        pairs = [(i, (i + shift) % cores) for i in range(cores)]
        all_sums = all_sums + lax.ppermute(row_sums, "tensor", pairs)
    gradient_sum, weighted_gradient_sum = all_sums[0], all_sums[1]
    grad_own = lax.dynamic_slice_in_dim(residual_gradient, column_offset, shard_width, 1)
    grad_tokens = grad_own + first_inverse_deviation * (
        centered_gradient
        - gradient_sum[:, None] / total_width
        - owned_normalized * (weighted_gradient_sum[:, None] / total_width)
    )
    first_gain_gradient = jnp.sum(first_normed_gradient * owned_normalized, axis=0)
    gbb_one = jnp.sum(first_normed_gradient, axis=0)
    vectors = (
        first_gain_gradient,
        gbb_one,
        gq_bias,
        gv_bias,
        gb_o,
        second_gain_gradient,
        gbb_two,
        gb_fc,
        gb_pr,
    )
    packed = jnp.concatenate([piece.reshape(groups, 1, -1) for piece in vectors], axis=2)
    chunks = qkv_chunks + [o_chunk] + pr_chunks + fc_chunks
    chunks.append(split_blocks(packed, groups, Y_FIRST))
    own_q, own_k, own_v, own_o, pr_top, pr_bottom, fc_left, fc_right, own_vectors = reduce_blocks(
        chunks
    )
    own_qkv = jnp.stack([own_q, own_k, own_v], axis=1)
    own_pr = jnp.concatenate([pr_top, pr_bottom], axis=0)
    own_fc = jnp.concatenate([fc_left, fc_right], axis=1)
    own_vectors = own_vectors[0]
    pieces = []
    offset = 0
    for piece in vectors:
        length = piece.shape[0] // groups
        pieces.append(own_vectors[offset : offset + length])
        offset += length
    gain_one, bias_one, q_own, v_own, o_own, gain_two, bias_two, fc_own, pr_own = pieces
    return (
        block_out,
        grad_tokens,
        gain_one,
        bias_one,
        own_qkv,
        q_own,
        v_own,
        own_o,
        o_own,
        gain_two,
        bias_two,
        own_fc,
        fc_own,
        own_pr,
        pr_own,
    )


def solution(mesh):
    placed = (
        P("dp", "tensor"),
        P("dp"),
        P(),
        P(),
        P(None, None, "tensor"),
        P("tensor"),
        P("tensor"),
        P("tensor", None),
        P(),
        P(),
        P(),
        P(None, "tensor"),
        P("tensor"),
        P("tensor", None),
        P(),
        P("dp", "tensor"),
    )
    return jax.shard_map(
        body,
        mesh=mesh,
        in_specs=placed,
        out_specs=(
            P("dp", "tensor"),
            P("dp", "tensor"),
            P(("tensor", "dp")),
            P(("tensor", "dp")),
            P("dp", None, "tensor"),
            P(("tensor", "dp")),
            P(("tensor", "dp")),
            P(("tensor", "dp"), None),
            P("dp"),
            P("dp"),
            P("dp"),
            P("dp", "tensor"),
            P(("tensor", "dp")),
            P(("tensor", "dp"), None),
            P("dp"),
        ),
        check_vma=False,
    )
```
